32 devices in a mesh: sample: 2 (over core), slab: 16 (over z, y, x).
Axes of the slice: x: 2, y: 2, z: 4, core: 2. Of those that a mesh axis runs over, the one named last changes fastest.
Arguments:
- force: float32 [3, 64, 32, 256], P(None, 'slab', None, 'sample'), parts along dimension 3, may hold values from -8 to 8, as said below
- modulus: float32 [64, 32, 256], P('slab', None, 'sample'), parts along dimension 2, may hold values from 0.2 to 1
Outputs:
- fine_field: float32 [3, 64, 32, 256], P(None, 'slab', None, 'sample'), parts along dimension 3
- coarse_field: float32 [3, 32, 16, 128], P(None, 'slab', None, 'sample'), parts along dimension 3
- compliance: float32 [4], P('sample'), parts along dimension 0
The draws below stay inside these ranges and needn't reach their ends.
There are 2 independent parts, one for each index of `sample`. The reference program is written for one: setup_inputs(seed, part) draws one part's arguments, and reference() takes and returns one part's arrays. A program takes and returns all parts, laid end to end along the dimension named above; each array names one. Nothing has to cross between parts.
Inputs may be any that keep to these rules, and one draw needn't show every extreme that they name: Body force on each cell and component.
All inputs are finite; a program needn't handle non-finite values.
Results may differ from the reference program's by a relative error of at most 0.0001.
Values sent between devices are 32-bit elements; how exact they have to be, the bound alone decides.
A program may use at most 128 MiB of HBM per device.

```python
import math
import jax
import jax.numpy as jnp
from jax import lax

NX = 128
NY = 32
ITERS = 2
SMOOTH = 2
CDEG = 4
NZ = 64


def draw_force(key, part):
    noise_key = jax.random.fold_in(key, 11)
    depth = jnp.arange(NZ, dtype=jnp.float32) / float(max(NZ - 1, 1))
    ramp = (0.5 + 1.5 * depth)[None, :, None, None]
    base = jax.random.truncated_normal(noise_key, -4.0, 4.0, (3, NZ, NY, NX), jnp.float32)
    return (base * ramp).astype(jnp.float32)


def block_levels(rng, shape, pieces, smallest, largest):
    def one(dim, parts):
        steps = jax.random.uniform(jax.random.fold_in(jax.random.fold_in(rng, 6), dim), (parts,), jnp.float32, smallest / len(pieces), largest / len(pieces))
        return jnp.repeat(jnp.exp(steps), shape[dim] // parts).reshape((-1,) + (1,) * (len(shape) - dim - 1))

    factor_of = one(*pieces[0])
    for cut in pieces[1:]:
        factor_of = factor_of * one(*cut)
    return factor_of


def setup_inputs(seed: int = 0, part: int = 0) -> dict:
    arg_keys = jax.random.split(jax.random.key(seed), 3)
    own_keys = jax.random.split(jax.random.fold_in(arg_keys[2], part), 3)
    return {
        "force": draw_force(jax.random.fold_in(jax.random.fold_in(arg_keys[2], part), 71), part),
        "modulus": jnp.clip(jnp.exp(math.log(1.0) - 1.609438 * jax.random.uniform(own_keys[1], (NZ, NY, NX), jnp.float32) ** block_levels(own_keys[1], (NZ, NY, NX), ((0, 16),), -0.2, 0.2)), 0.2, 1.0),
    }


def shift_back(values, dimension):
    length = values.shape[dimension]
    zeroes = jnp.zeros_like(lax.slice_in_dim(values, 0, 1, axis=dimension))
    return jnp.concatenate([zeroes, lax.slice_in_dim(values, 0, length - 1, axis=dimension)], axis=dimension)


def shift_ahead(values, dimension):
    length = values.shape[dimension]
    zeroes = jnp.zeros_like(lax.slice_in_dim(values, 0, 1, axis=dimension))
    return jnp.concatenate([lax.slice_in_dim(values, 1, length, axis=dimension), zeroes], axis=dimension)


def operate(displace, lame):
    grad_z = shift_ahead(displace, 1) - displace
    grad_y = shift_ahead(displace, 2) - displace
    grad_x = shift_ahead(displace, 3) - displace
    spread = lame * (grad_x[0] + grad_y[1] + grad_z[2])
    flux_z = lame * grad_z
    flux_y = lame * grad_y
    flux_x = lame * grad_x
    result = (shift_back(flux_z, 1) - flux_z) + (shift_back(flux_y, 2) - flux_y) + (shift_back(flux_x, 3) - flux_x)
    pressure = jnp.stack([shift_back(spread, 2) - spread, shift_back(spread, 1) - spread, shift_back(spread, 0) - spread])
    return result + pressure


def diag_inverse(lame):
    laplace = (lame + shift_back(lame, 0)) + (lame + shift_back(lame, 1)) + (lame + shift_back(lame, 2))
    diagonal = jnp.stack([laplace + lame + shift_back(lame, 2), laplace + lame + shift_back(lame, 1), laplace + lame + shift_back(lame, 0)])
    return 1.0 / diagonal


def restrict_scalar(values):
    shape = values.shape
    return values.reshape(shape[0] // 2, 2, shape[1] // 2, 2, shape[2] // 2, 2).mean(axis=(1, 3, 5))


def restrict_vector(values):
    shape = values.shape
    return values.reshape(shape[0], shape[1] // 2, 2, shape[2] // 2, 2, shape[3] // 2, 2).mean(axis=(2, 4, 6))


def prolong(values):
    return jnp.repeat(jnp.repeat(jnp.repeat(values, 2, 1), 2, 2), 2, 3)


def chebyshev(iterate, residue, operator, inverse, degree, low_end, high_end):
    centre = (high_end + low_end) / 2.0
    half_width = (high_end - low_end) / 2.0
    spread_ratio = centre / half_width
    rho_now = 1.0 / spread_ratio
    update = inverse * residue / centre
    for section in range(degree):
        iterate = iterate + update
        residue = residue - operator(update)
        if section + 1 < degree:
            rho_next = 1.0 / (2.0 * spread_ratio - rho_now)
            update = rho_next * rho_now * update + (2.0 * rho_next / half_width) * (inverse * residue)
            rho_now = rho_next
    return iterate, residue


def reference(force, modulus):
    lame = 0.4 * modulus
    coarse_lame = restrict_scalar(lame)
    fine_inverse = diag_inverse(lame)
    coarse_inverse = diag_inverse(coarse_lame)

    def fine_operator(vector):
        return operate(vector, lame)

    def coarse_operator(vector):
        return operate(vector, coarse_lame)

    iterate = jnp.zeros_like(force)
    residue = force
    for cycle in range(ITERS):
        iterate, residue = chebyshev(iterate, residue, fine_operator, fine_inverse, SMOOTH, 0.25, 2.0)
        coarse_rhs = 4.0 * restrict_vector(residue)
        correction, unused = chebyshev(jnp.zeros_like(coarse_rhs), coarse_rhs, coarse_operator, coarse_inverse, CDEG, 0.02, 2.0)
        expanded = prolong(correction)
        iterate = iterate + expanded
        residue = residue - fine_operator(expanded)
        iterate, residue = chebyshev(iterate, residue, fine_operator, fine_inverse, SMOOTH, 0.25, 2.0)
    coarse_force = restrict_vector(force)
    coarse_field, unused = chebyshev(jnp.zeros_like(coarse_force), 4.0 * coarse_force, coarse_operator, coarse_inverse, 2 * CDEG, 0.02, 2.0)
    cells = float(NX * NY * NZ)
    compliance = jnp.stack([jnp.sum(force * iterate) / cells, jnp.sum(coarse_force * coarse_field) / (cells / 8.0)])
    return iterate, coarse_field, compliance
```

```python
import functools

import jax
import jax.numpy as jnp
from jax import lax
from jax.experimental import pallas as pl
from jax.experimental.pallas import tpu as pltpu
from jax.sharding import PartitionSpec as P

CDEG = 4
FINE = (0.25, 2.0)
COARSE = (0.02, 2.0)
H = 8
U_FINE = 1
U_COARSE = 1


def coefficients(low, high, degree):
    centre, half = (high + low) / 2.0, (high - low) / 2.0
    ratio = centre / half
    rho = 1.0 / ratio
    steps = []
    for _ in range(degree - 1):
        nxt = 1.0 / (2.0 * ratio - rho)
        steps.append((nxt * rho, 2.0 * nxt / half))
        rho = nxt
    return 1.0 / centre, steps


def shifts(rows, lanes, step):
    lane = lax.broadcasted_iota(jnp.int32, (rows, lanes), 1)
    row = lax.broadcasted_iota(jnp.int32, (rows, lanes), 0)

    def ahead_x(u):
        return jnp.where(lane < lanes - step, pltpu.roll(u, lanes - step, 1), 0.0)

    def back_x(u):
        return jnp.where(lane >= step, pltpu.roll(u, step, 1), 0.0)

    def ahead_y(u):
        return jnp.where(row < rows - 1, pltpu.roll(u, rows - 1, 0), 0.0)

    def back_y(u):
        return jnp.where(row >= 1, pltpu.roll(u, 1, 0), 0.0)

    return ahead_x, back_x, ahead_y, back_y


def loop(lo, hi, body, carry, unroll):
    return lax.fori_loop(lo + H, hi + H, body, carry, unroll=unroll)


def invert(lam, inv, lo, hi, first, last, sh, unroll):
    _, back_x, _, back_y = sh

    def body(z, below):
        m = lam[z]
        mx, my = back_x(m), back_y(m)
        base = (m + below) + (m + my) + (m + mx) + m
        live = jnp.logical_and(z - H >= first, z - H < last)
        for c, extra in enumerate((mx, my, below)):
            inv[c, z] = jnp.where(live, 1.0 / (base + extra), 0.0)
        return m

    loop(lo, hi, body, lam[lo - 1 + H], unroll)


def begin(src, inv, w, x, lo, hi, scale, unroll):
    def body(z, carry):
        for c in range(3):
            v = inv[c, z] * src[c, z] * scale
            w[c, z] = v
            if x is not None:
                x[c, z] = v
        return carry

    loop(lo, hi, body, 0, unroll)


def sweep(src, r, w, x, lam, inv, lo, hi, old, new, sh, unroll):
    ahead_x, back_x, ahead_y, back_y = sh

    def upward(z, u, div):
        m = lam[z]
        gz = [w[c, z + 1] - u[c] for c in range(3)]
        s = m * (div + gz[2])
        return [m * gz[0], m * gz[1], m * gz[2] + s], s, m

    def spread(u):
        return (ahead_x(u[0]) - u[0]) + (ahead_y(u[1]) - u[1])

    def body(z, below):
        u = [w[c, z] for c in range(3)]
        gx = [ahead_x(v) - v for v in u]
        gy = [ahead_y(v) - v for v in u]
        up, s, m = upward(z, u, gx[0] + gy[1])
        fx = [m * g for g in gx]
        fy = [m * g for g in gy]
        fx[0] = fx[0] + s
        fy[1] = fy[1] + s
        for c in range(3):
            a = (below[c] - up[c]) + (back_y(fy[c]) - fy[c]) + (back_x(fx[c]) - fx[c])
            rest = src[c, z] - a
            r[c, z] = rest
            if new is not None:
                v = new * (inv[c, z] * rest)
                if old is not None:
                    v = old * u[c] + v
                w[c, z] = v
                if x is not None:
                    x[c, z] = x[c, z] + v
        return tuple(up)

    z0 = lo - 1 + H
    u0 = [w[c, z0] for c in range(3)]
    up0, _, _ = upward(z0, u0, spread(u0))
    loop(lo, hi, body, tuple(up0), unroll)


def pack(load, tmp, scale, even):
    lanes = even.shape[1]
    halves = []
    for k in range(2):
        tmp[k] = load(2 * k) + load(2 * k + 1)
        n = even.shape[0]
        halves.append(tmp[k, pl.ds(0, n, stride=2), :] + tmp[k, pl.ds(1, n, stride=2), :])
    a, b = halves
    return scale * jnp.where(even, a + pltpu.roll(a, lanes - 1, 1), b + pltpu.roll(b, 1, 1))


def unpack(p, even):
    lanes = even.shape[1]
    return jnp.where(even, p, pltpu.roll(p, 1, 1)), jnp.where(even, pltpu.roll(p, lanes - 1, 1), p)


def kernel(n, L, force, modulus, out, cout, comp, fm, lam, inv, r, w, x, tmp, cg, c1, c2, clam, cinv, cf, cr, cw, ce, part, lsem, ssem, rsem, sums_s, sums_r):
    me = lax.axis_index("slab")
    rows, lanes = fm.shape[2], fm.shape[3]
    crows = rows // 2
    barrier = pltpu.get_barrier_semaphore()

    def greet(k, carry):
        pl.semaphore_signal(barrier, inc=1, device_id={"slab": lax.rem(me + k, n)}, device_id_type=pl.DeviceIdType.MESH)
        return carry

    lax.fori_loop(1, n, greet, 0)
    own = pl.ds(H, L)
    loads = [
        pltpu.make_async_copy(force, fm.at[pl.ds(0, 3), own], lsem.at[0]),
        pltpu.make_async_copy(modulus, fm.at[3, own], lsem.at[1]),
    ]
    for cp in loads:
        cp.start()

    copies = {}

    def remote(name, src, dst, d):
        i = len(copies)
        copies[name] = (
            pltpu.make_async_remote_copy(
                src_ref=src, dst_ref=dst, send_sem=ssem.at[i], recv_sem=rsem.at[i],
                device_id={"slab": me + d}, device_id_type=pl.DeviceIdType.MESH,
            ),
            d, dst,
        )

    def inside(i):
        return jnp.logical_and(i >= 0, i < n)

    def start(name):
        cp, d, _ = copies[name]
        pl.when(inside(me + d))(cp.start)

    def wait(name):
        cp, d, _ = copies[name]
        pl.when(inside(me - d))(cp.wait_recv)

    def clear(name):
        _, d, dst = copies[name]

        @pl.when(jnp.logical_not(inside(me - d)))
        def _():
            dst[...] = jnp.zeros(dst.shape, jnp.float32)

    def layers(name, d, lo, hi):
        mine = fm.at[:, pl.ds(H + lo, hi - lo)]
        theirs = fm.at[:, pl.ds(H + lo - d * L, hi - lo)]
        remote(name, mine, theirs, d)

    layers("near+", 1, 1, L)
    layers("near-", -1, 0, 2)
    layers("next+", 1, 0, 1)
    layers("next-", -1, 2, L)
    layers("far+", 2, 0, L)
    layers("far-", -2, 0, L - 1)
    for name, buf, reach in (("g", cg, 4), ("c1", c1, 3), ("c2", c2, 2)):
        for k in range(1, reach + 1):
            for d in (k, -k):
                remote((name, d), buf.at[reach], buf.at[reach - d], d)

    for name in copies:
        clear(name)

    even = lax.rem(lax.broadcasted_iota(jnp.int32, (crows, lanes), 1), 2) == 0
    fsh = shifts(rows, lanes, 1)
    csh = shifts(crows, lanes, 2)
    fscale, ((fold, fnew),) = coefficients(*FINE, 2)
    cscale, csteps = coefficients(*COARSE, CDEG)
    _, wsteps = coefficients(*COARSE, 2 * CDEG)

    for cp in loads:
        cp.wait()
    pl.semaphore_wait(barrier, n - 1)
    for name in ("near+", "near-"):
        start(name)
    for c in range(4):
        cg[4, c] = pack(lambda z: fm[c, H + z], tmp, 0.5 if c < 3 else 0.05, even)
    for k in range(1, 5):
        start(("g", k))
        start(("g", -k))
    for name in ("far+", "far-", "next+", "next-"):
        start(name)

    def take(lo, hi):
        def body(z, carry):
            lam[z] = 0.4 * fm[3, z]
            return carry

        loop(lo, hi, body, 0, U_FINE)

    first, last = -me * L, (n - me) * L
    cfirst, clast = -me * (L // 2), (n - me) * (L // 2)

    def exchange(name, buf, reach):
        for c in range(3):
            buf[reach, c] = pack(lambda z: r[c, H + z], tmp, 0.5, even)
        for k in range(1, reach + 1):
            start((name, k))
            start((name, -k))

    def gather(name, buf, reach, into):
        for k in range(1, reach + 1):
            wait((name, k))
            wait((name, -k))
        for d in range(-reach, reach + 1):
            for c in range(3):
                a, b = unpack(buf[reach + d, c], even)
                into[c, H + 2 * d] = a
                into[c, H + 2 * d + 1] = b

    wait("near+")
    wait("near-")
    take(-3, L + 2)
    invert(lam, inv, -2, L + 2, first, last, fsh, U_FINE)
    begin(fm, inv, w, None, -2, L + 2, fscale, U_FINE)
    sweep(fm, r, w, None, lam, inv, -1, L + 1, fold, fnew, fsh, U_FINE)
    sweep(r, r, w, None, lam, inv, 0, L, None, None, fsh, U_FINE)
    exchange("c1", c1, 3)

    for k in range(1, 5):
        wait(("g", k))
        wait(("g", -k))
    for d in range(-4, 5):
        for c in range(4):
            a, b = unpack(cg[4 + d, c], even)
            for z, v in ((H + 2 * d, a), (H + 2 * d + 1, b)):
                if c < 3:
                    cf[c, z] = v
                else:
                    clam[z] = v
    invert(clam, cinv, -7, 9, cfirst, clast, csh, U_COARSE)
    for name in ("far+", "far-", "next+", "next-"):
        wait(name)
    take(-8, -3)
    take(L + 2, L + 7)
    invert(lam, inv, -7, -2, first, last, fsh, U_FINE)
    invert(lam, inv, L + 2, L + 7, first, last, fsh, U_FINE)
    begin(fm, inv, w, x, -7, L + 7, fscale, U_FINE)
    sweep(fm, r, w, x, lam, inv, -6, L + 6, fold, fnew, fsh, U_FINE)
    sweep(r, r, w, None, lam, inv, -5, L + 5, None, None, fsh, U_FINE)

    def solve(lo, hi, rhs, steps):
        begin(rhs, cinv, cw, ce, lo, hi, cscale, U_COARSE)
        for k, (old, new) in enumerate(steps):
            src = rhs if k == 0 else cr
            sweep(src, cr, cw, ce, clam, cinv, lo + k + 1, hi - k - 1, old, new, csh, U_COARSE)

    def prolong(lo, hi):
        def body(z, carry):
            for c in range(3):
                e = ce[c, z]
                for half in range(2):
                    f = 2 * (z - H) + half + H
                    w[c, f, pl.ds(0, crows, stride=2), :] = e
                    w[c, f, pl.ds(1, crows, stride=2), :] = e
                    x[c, f] = x[c, f] + w[c, f]
            return carry

        loop(lo, hi, body, 0, U_COARSE)

    gather("c1", c1, 3, cr)
    solve(-6, 8, cr, csteps)
    prolong(-3, 5)
    sweep(r, r, w, x, lam, inv, -5, L + 5, None, fscale, fsh, U_FINE)
    sweep(r, r, w, x, lam, inv, -4, L + 4, fold, fnew, fsh, U_FINE)
    sweep(r, r, w, x, lam, inv, -3, L + 3, None, fscale, fsh, U_FINE)
    sweep(r, r, w, x, lam, inv, -2, L + 2, fold, fnew, fsh, U_FINE)
    sweep(r, r, w, None, lam, inv, -1, L + 1, None, None, fsh, U_FINE)
    exchange("c2", c2, 2)

    solve(-7, 9, cf, wsteps)
    coarse_sum = jnp.zeros((crows, lanes), jnp.float32)
    pick = (
        lax.broadcasted_iota(jnp.int32, (lanes, lanes // 2), 0)
        == 2 * lax.broadcasted_iota(jnp.int32, (lanes, lanes // 2), 1)
    ).astype(jnp.float32)
    for c in range(3):
        for z in range(L // 2):
            v = ce[c, H + z]
            coarse_sum = coarse_sum + v * cf[c, H + z]
            cout[c, z] = jnp.dot(v, pick, precision=lax.Precision.HIGHEST, preferred_element_type=jnp.float32)

    gather("c2", c2, 2, cr)
    solve(-4, 6, cr, csteps)
    prolong(-1, 3)
    sweep(r, r, w, x, lam, inv, -1, L + 1, None, fscale, fsh, U_FINE)
    sweep(r, r, w, x, lam, inv, 0, L, fold, fnew, fsh, U_FINE)

    fine_sum = jnp.zeros((rows, lanes), jnp.float32)
    for c in range(3):
        for z in range(L):
            v = x[c, H + z]
            out[c, z] = v
            fine_sum = fine_sum + v * fm[c, H + z]
    part[0, 0:1] = jnp.sum(fine_sum, axis=0, keepdims=True)
    part[0, 1:2] = jnp.sum(coarse_sum, axis=0, keepdims=True)

    def tell(k):
        return pltpu.make_async_remote_copy(
            src_ref=part.at[0], dst_ref=part.at[k], send_sem=sums_s.at[k], recv_sem=sums_r.at[k],
            device_id={"slab": lax.rem(me + k, n)}, device_id_type=pl.DeviceIdType.MESH,
        )

    def say(k, carry):
        tell(k).start()
        return carry

    def hear(k, carry):
        tell(k).wait_recv()
        return carry

    lax.fori_loop(1, n, say, 0)
    for name in copies:
        cp, d, _ = copies[name]
        pl.when(inside(me + d))(cp.wait_send)
    lax.fori_loop(1, n, hear, 0)
    total = jnp.sum(part[...], axis=0)
    cells = 1.0 / (n * L * rows * lanes)
    comp[0] = jnp.sum(total[0:1]) * cells
    comp[1] = jnp.sum(total[1:2]) * cells

    def done(k, carry):
        tell(k).wait_send()
        return carry

    lax.fori_loop(1, n, done, 0)


def body(n, force, modulus):
    _, L, rows, lanes = force.shape
    f32 = jnp.float32
    fine, coarse = (L + 2 * H, rows, lanes), (L // 2 + 2 * H, rows // 2, lanes)
    pair = (rows // 2, lanes)
    V = pltpu.VMEM
    remotes = 6 + 8 + 6 + 4
    scratch = [
        V((4,) + fine, f32), V(fine, f32), V((3,) + fine, f32), V((3,) + fine, f32),
        V((3,) + fine, f32), V((3,) + fine, f32), V((2, rows, lanes), f32),
        V((9, 4) + pair, f32), V((7, 3) + pair, f32), V((5, 3) + pair, f32),
        V(coarse, f32), V((3,) + coarse, f32), V((3,) + coarse, f32), V((3,) + coarse, f32),
        V((3,) + coarse, f32), V((3,) + coarse, f32), V((n, 2, lanes), f32),
        pltpu.SemaphoreType.DMA((2,)),
        pltpu.SemaphoreType.DMA((remotes,)), pltpu.SemaphoreType.DMA((remotes,)),
        pltpu.SemaphoreType.DMA((n,)), pltpu.SemaphoreType.DMA((n,)),
    ]
    vmem = pl.BlockSpec(memory_space=pltpu.VMEM)
    return pl.pallas_call(
        functools.partial(kernel, n, L),
        out_shape=(
            jax.ShapeDtypeStruct(force.shape, f32),
            jax.ShapeDtypeStruct((3, L // 2, rows // 2, lanes // 2), f32),
            jax.ShapeDtypeStruct((2,), f32),
        ),
        in_specs=[pl.BlockSpec(memory_space=pl.ANY)] * 2,
        out_specs=(vmem, vmem, pl.BlockSpec(memory_space=pltpu.SMEM)),
        scratch_shapes=scratch,
        compiler_params=pltpu.CompilerParams(collective_id=0, has_side_effects=True),
    )(force, modulus)


def solution(mesh):
    return jax.shard_map(
        functools.partial(body, mesh.shape["slab"]),
        mesh=mesh,
        in_specs=(P(None, "slab", None, "sample"), P("slab", None, "sample")),
        out_specs=(P(None, "slab", None, "sample"), P(None, "slab", None, "sample"), P("sample")),
        check_vma=False,
    )
```

```python
import functools

import jax
import jax.numpy as jnp
from jax import lax
from jax.experimental import pallas as pl
from jax.experimental.pallas import tpu as pltpu
from jax.sharding import PartitionSpec as P

CDEG = 4
FINE = (0.25, 2.0)
COARSE = (0.02, 2.0)
H = 8
REACH = 4
U_FINE = True
U_COARSE = True


def rounds(n):
    count = 0
    while REACH * 2**count < n - 1:
        count += 1
    return count


def coefficients(low, high, degree):
    centre, half = (high + low) / 2.0, (high - low) / 2.0
    ratio = centre / half
    rho = 1.0 / ratio
    steps = []
    for _ in range(degree - 1):
        nxt = 1.0 / (2.0 * ratio - rho)
        steps.append((nxt * rho, 2.0 * nxt / half))
        rho = nxt
    return 1.0 / centre, steps


def shifts(rows, lanes, step):
    lane = lax.broadcasted_iota(jnp.int32, (rows, lanes), 1)
    row = lax.broadcasted_iota(jnp.int32, (rows, lanes), 0)

    def ahead_x(u):
        return jnp.where(lane < lanes - step, pltpu.roll(u, lanes - step, 1), 0.0)

    def back_x(u):
        return jnp.where(lane >= step, pltpu.roll(u, step, 1), 0.0)

    def ahead_y(u):
        return jnp.where(row < rows - 1, pltpu.roll(u, rows - 1, 0), 0.0)

    def back_y(u):
        return jnp.where(row >= 1, pltpu.roll(u, 1, 0), 0.0)

    return ahead_x, back_x, ahead_y, back_y


def loop(lo, hi, body, carry, unroll):
    return lax.fori_loop(lo + H, hi + H, body, carry, unroll=unroll)


def invert(lam, inv, lo, hi, first, last, sh, unroll):
    _, back_x, _, back_y = sh

    def body(z, below):
        m = lam[z]
        mx, my = back_x(m), back_y(m)
        base = (m + below) + (m + my) + (m + mx) + m
        live = jnp.logical_and(z - H >= first, z - H < last)
        for c, extra in enumerate((mx, my, below)):
            inv[c, z] = jnp.where(live, 1.0 / (base + extra), 0.0)
        return m

    loop(lo, hi, body, lam[lo - 1 + H], unroll)


def begin(src, inv, w, x, lo, hi, scale, unroll):
    def body(z, carry):
        for c in range(3):
            v = inv[c, z] * src[c, z] * scale
            w[c, z] = v
            if x is not None:
                x[c, z] = v
        return carry

    loop(lo, hi, body, 0, unroll)


def sweep(src, r, w, x, lam, inv, lo, hi, old, new, sh, unroll):
    ahead_x, back_x, ahead_y, back_y = sh

    def upward(z, u, div):
        m = lam[z]
        gz = [w[c, z + 1] - u[c] for c in range(3)]
        s = m * (div + gz[2])
        return [m * gz[0], m * gz[1], m * gz[2] + s], s, m

    def spread(u):
        return (ahead_x(u[0]) - u[0]) + (ahead_y(u[1]) - u[1])

    def body(z, below):
        u = [w[c, z] for c in range(3)]
        gx = [ahead_x(v) - v for v in u]
        gy = [ahead_y(v) - v for v in u]
        up, s, m = upward(z, u, gx[0] + gy[1])
        fx = [m * g for g in gx]
        fy = [m * g for g in gy]
        fx[0] = fx[0] + s
        fy[1] = fy[1] + s
        for c in range(3):
            a = (below[c] - up[c]) + (back_y(fy[c]) - fy[c]) + (back_x(fx[c]) - fx[c])
            rest = src[c, z] - a
            r[c, z] = rest
            if new is not None:
                v = new * (inv[c, z] * rest)
                if old is not None:
                    v = old * u[c] + v
                w[c, z] = v
                if x is not None:
                    x[c, z] = x[c, z] + v
        return tuple(up)

    z0 = lo - 1 + H
    u0 = [w[c, z0] for c in range(3)]
    up0, _, _ = upward(z0, u0, spread(u0))
    loop(lo, hi, body, tuple(up0), unroll)


def pack(load, tmp, scale, even):
    lanes = even.shape[1]
    halves = []
    for k in range(2):
        tmp[k] = load(2 * k) + load(2 * k + 1)
        n = even.shape[0]
        halves.append(tmp[k, pl.ds(0, n, stride=2), :] + tmp[k, pl.ds(1, n, stride=2), :])
    a, b = halves
    return scale * jnp.where(even, a + pltpu.roll(a, lanes - 1, 1), b + pltpu.roll(b, 1, 1))


def unpack(p, even):
    lanes = even.shape[1]
    return jnp.where(even, p, pltpu.roll(p, 1, 1)), jnp.where(even, pltpu.roll(p, lanes - 1, 1), p)


def kernel(n, L, force, modulus, out, cout, comp, fm, lam, inv, r, w, x, tmp, cg, c1, c2, clam, cinv, cf, cr, cw, ce, part, known, lsem, ssem, rsem, sums_s, sums_r):
    me = lax.axis_index("slab")
    rows, lanes = fm.shape[2], fm.shape[3]
    crows = rows // 2
    barrier = pltpu.get_barrier_semaphore()

    def inside(i):
        return jnp.logical_and(i >= 0, i < n)

    def signal(sem, d):
        @pl.when(inside(me + d))
        def _():
            pl.semaphore_signal(sem, inc=1, device_id={"slab": me + d}, device_id_type=pl.DeviceIdType.MESH)

    greeted = 0
    for k in range(1, REACH + 1):
        for d in (k, -k):
            signal(barrier, d)
            greeted = greeted + inside(me + d).astype(jnp.int32)

    def round_tell(j):
        signal(known.at[2 * j], REACH * 2**j)
        signal(known.at[2 * j + 1], -REACH * 2**j)

    def round_hear(j):
        pl.when(inside(me - REACH * 2**j))(lambda: pl.semaphore_wait(known.at[2 * j], 1))
        pl.when(inside(me + REACH * 2**j))(lambda: pl.semaphore_wait(known.at[2 * j + 1], 1))

    own = pl.ds(H, L)
    loads = [
        pltpu.make_async_copy(force, fm.at[pl.ds(0, 3), own], lsem.at[0]),
        pltpu.make_async_copy(modulus, fm.at[3, own], lsem.at[1]),
    ]
    for cp in loads:
        cp.start()

    copies = {}

    def remote(name, src, dst, d):
        i = len(copies)
        copies[name] = (
            pltpu.make_async_remote_copy(
                src_ref=src, dst_ref=dst, send_sem=ssem.at[i], recv_sem=rsem.at[i],
                device_id={"slab": me + d}, device_id_type=pl.DeviceIdType.MESH,
            ),
            d, dst,
        )

    def start(name):
        cp, d, _ = copies[name]
        pl.when(inside(me + d))(cp.start)

    def wait(name):
        cp, d, _ = copies[name]
        pl.when(inside(me - d))(cp.wait_recv)

    def clear(name):
        _, d, dst = copies[name]

        @pl.when(jnp.logical_not(inside(me - d)))
        def _():
            dst[...] = jnp.zeros(dst.shape, jnp.float32)

    def layers(name, d, part, lo, hi):
        mine = fm.at[part, pl.ds(H + lo, hi - lo)]
        theirs = fm.at[part, pl.ds(H + lo - d * L, hi - lo)]
        remote(name, mine, theirs, d)

    force3, both = pl.ds(0, 3), pl.ds(0, 4)
    layers("near+", 1, force3, 2, L)
    layers("near+m", 1, 3, 1, L)
    layers("near-", -1, both, 0, 2)
    layers("next+", 1, force3, 0, 2)
    layers("next+m", 1, 3, 0, 1)
    layers("next-", -1, both, 2, L)
    layers("far+", 2, force3, 1, L)
    layers("far+m", 2, 3, 0, L)
    layers("far-", -2, both, 0, L - 1)
    for name, buf, reach in (("g", cg, 4), ("c1", c1, 3), ("c2", c2, 2)):
        for k in range(2 if name == "g" else 1, reach + 1):
            for d in (k, -k):
                remote((name, d), buf.at[reach], buf.at[reach - d], d)

    for name in copies:
        clear(name)

    even = lax.rem(lax.broadcasted_iota(jnp.int32, (crows, lanes), 1), 2) == 0
    fsh = shifts(rows, lanes, 1)
    csh = shifts(crows, lanes, 2)
    fscale, ((fold, fnew),) = coefficients(*FINE, 2)
    cscale, csteps = coefficients(*COARSE, CDEG)
    _, wsteps = coefficients(*COARSE, 2 * CDEG)

    near = ("near+", "near+m", "near-")
    rest = ("next+", "next+m", "next-")
    far = ("far+", "far+m", "far-")
    for cp in loads:
        cp.wait()
    pl.semaphore_wait(barrier, greeted)
    round_tell(0)
    for name in near:
        start(name)
    for name in rest:
        start(name)

    def reduced(d):
        for c in range(4):
            cg[4 + d, c] = pack(lambda z: fm[c, H + d * L + z], tmp, 0.5 if c < 3 else 0.05, even)

    reduced(0)
    for k in range(2, 5):
        start(("g", k))
        start(("g", -k))
    for name in far:
        start(name)

    def take(lo, hi):
        def body(z, carry):
            lam[z] = 0.4 * fm[3, z]
            return carry

        loop(lo, hi, body, 0, U_FINE)

    first, last = -me * L, (n - me) * L
    cfirst, clast = -me * (L // 2), (n - me) * (L // 2)

    def exchange(name, buf, reach):
        for c in range(3):
            buf[reach, c] = pack(lambda z: r[c, H + z], tmp, 0.5, even)
        for k in range(1, reach + 1):
            start((name, k))
            start((name, -k))

    def gather(name, buf, reach, into):
        for k in range(1, reach + 1):
            wait((name, k))
            wait((name, -k))
        for d in range(-reach, reach + 1):
            for c in range(3):
                a, b = unpack(buf[reach + d, c], even)
                into[c, H + 2 * d] = a
                into[c, H + 2 * d + 1] = b

    for name in near:
        wait(name)
    take(-3, L + 2)
    invert(lam, inv, -2, L + 2, first, last, fsh, U_FINE)
    begin(fm, inv, w, None, -2, L + 2, fscale, U_FINE)
    sweep(fm, r, w, None, lam, inv, -1, L + 1, fold, fnew, fsh, U_FINE)
    sweep(r, r, w, None, lam, inv, 0, L, None, None, fsh, U_FINE)
    exchange("c1", c1, 3)

    def solve(lo, hi, rhs, steps):
        begin(rhs, cinv, cw, ce, lo, hi, cscale, U_COARSE)
        for k, (old, new) in enumerate(steps):
            src = rhs if k == 0 else cr
            sweep(src, cr, cw, ce, clam, cinv, lo + k + 1, hi - k - 1, old, new, csh, U_COARSE)

    def prolong(lo, hi):
        def body(z, carry):
            for c in range(3):
                e = ce[c, z]
                for half in range(2):
                    f = 2 * (z - H) + half + H
                    w[c, f, pl.ds(0, crows, stride=2), :] = e
                    w[c, f, pl.ds(1, crows, stride=2), :] = e
                    x[c, f] = x[c, f] + w[c, f]
            return carry

        loop(lo, hi, body, 0, U_COARSE)

    for name in rest:
        wait(name)
    reduced(-1)
    reduced(1)
    for k in range(2, 5):
        wait(("g", k))
        wait(("g", -k))
    for d in range(-4, 5):
        for c in range(4):
            a, b = unpack(cg[4 + d, c], even)
            for z, v in ((H + 2 * d, a), (H + 2 * d + 1, b)):
                if c < 3:
                    cf[c, z] = v
                else:
                    clam[z] = v
    invert(clam, cinv, -7, 9, cfirst, clast, csh, U_COARSE)
    gather("c1", c1, 3, cr)
    solve(-6, 8, cr, csteps)

    for name in far:
        wait(name)
    take(-8, -3)
    take(L + 2, L + 7)
    invert(lam, inv, -7, -2, first, last, fsh, U_FINE)
    invert(lam, inv, L + 2, L + 7, first, last, fsh, U_FINE)
    begin(fm, inv, w, x, -7, L + 7, fscale, U_FINE)
    sweep(fm, r, w, x, lam, inv, -6, L + 6, fold, fnew, fsh, U_FINE)
    sweep(r, r, w, None, lam, inv, -5, L + 5, None, None, fsh, U_FINE)

    prolong(-3, 5)
    sweep(r, r, w, x, lam, inv, -5, L + 5, None, fscale, fsh, U_FINE)
    sweep(r, r, w, x, lam, inv, -4, L + 4, fold, fnew, fsh, U_FINE)
    sweep(r, r, w, x, lam, inv, -3, L + 3, None, fscale, fsh, U_FINE)
    sweep(r, r, w, x, lam, inv, -2, L + 2, fold, fnew, fsh, U_FINE)
    sweep(r, r, w, None, lam, inv, -1, L + 1, None, None, fsh, U_FINE)
    exchange("c2", c2, 2)

    for j in range(1, rounds(n)):
        round_hear(j - 1)
        round_tell(j)

    solve(-7, 9, cf, wsteps)
    coarse_sum = jnp.zeros((crows, lanes), jnp.float32)
    pick = (
        lax.broadcasted_iota(jnp.int32, (lanes, lanes // 2), 0)
        == 2 * lax.broadcasted_iota(jnp.int32, (lanes, lanes // 2), 1)
    ).astype(jnp.float32)
    for c in range(3):
        for z in range(L // 2):
            v = ce[c, H + z]
            coarse_sum = coarse_sum + v * cf[c, H + z]
            cout[c, z] = jnp.dot(v, pick, precision=lax.Precision.HIGHEST, preferred_element_type=jnp.float32)

    gather("c2", c2, 2, cr)
    solve(-4, 6, cr, csteps)
    prolong(-1, 3)
    sweep(r, r, w, x, lam, inv, -1, L + 1, None, fscale, fsh, U_FINE)
    sweep(r, r, w, x, lam, inv, 0, L, fold, fnew, fsh, U_FINE)

    fine_sum = jnp.zeros((rows, lanes), jnp.float32)
    for c in range(3):
        for z in range(L):
            v = x[c, H + z]
            out[c, z] = v
            fine_sum = fine_sum + v * fm[c, H + z]
    part[0, 0:1] = jnp.sum(fine_sum, axis=0, keepdims=True)
    part[0, 1:2] = jnp.sum(coarse_sum, axis=0, keepdims=True)

    def tell(k):
        return pltpu.make_async_remote_copy(
            src_ref=part.at[0], dst_ref=part.at[k], send_sem=sums_s.at[k], recv_sem=sums_r.at[k],
            device_id={"slab": lax.rem(me + k, n)}, device_id_type=pl.DeviceIdType.MESH,
        )

    def say(k, carry):
        tell(k).start()
        return carry

    def hear(k, carry):
        tell(k).wait_recv()
        return carry

    round_hear(rounds(n) - 1)
    lax.fori_loop(1, n, say, 0)
    for name in copies:
        cp, d, _ = copies[name]
        pl.when(inside(me + d))(cp.wait_send)
    lax.fori_loop(1, n, hear, 0)
    total = jnp.sum(part[...], axis=0)
    cells = 1.0 / (n * L * rows * lanes)
    comp[0] = jnp.sum(total[0:1]) * cells
    comp[1] = jnp.sum(total[1:2]) * cells

    def done(k, carry):
        tell(k).wait_send()
        return carry

    lax.fori_loop(1, n, done, 0)


def hand_out(fine, coarse, comp, fine_out, coarse_out, comp_out, sem):
    copies = [pltpu.make_async_copy(fine, fine_out, sem.at[0]), pltpu.make_async_copy(coarse, coarse_out, sem.at[1])]
    for cp in copies:
        cp.start()
    for i in range(2):
        comp_out[i] = comp[i]
    for cp in copies:
        cp.wait()


def body(n, force, modulus):
    _, L, rows, lanes = force.shape
    f32 = jnp.float32
    fine, coarse = (L + 2 * H, rows, lanes), (L // 2 + 2 * H, rows // 2, lanes)
    pair = (rows // 2, lanes)
    V = pltpu.VMEM
    remotes = 9 + 6 + 6 + 4
    scratch = [
        V((4,) + fine, f32), V(fine, f32), V((3,) + fine, f32), V((3,) + fine, f32),
        V((3,) + fine, f32), V((3,) + fine, f32), V((2, rows, lanes), f32),
        V((9, 4) + pair, f32), V((7, 3) + pair, f32), V((5, 3) + pair, f32),
        V(coarse, f32), V((3,) + coarse, f32), V((3,) + coarse, f32), V((3,) + coarse, f32),
        V((3,) + coarse, f32), V((3,) + coarse, f32), V((n, 2, lanes), f32),
        pltpu.SemaphoreType.REGULAR((2 * rounds(n),)),
        pltpu.SemaphoreType.DMA((2,)),
        pltpu.SemaphoreType.DMA((remotes,)), pltpu.SemaphoreType.DMA((remotes,)),
        pltpu.SemaphoreType.DMA((n,)), pltpu.SemaphoreType.DMA((n,)),
    ]
    vmem = pl.BlockSpec(memory_space=pltpu.VMEM)
    results = pl.pallas_call(
        functools.partial(kernel, n, L),
        out_shape=(
            jax.ShapeDtypeStruct(force.shape, f32),
            jax.ShapeDtypeStruct((3, L // 2, rows // 2, lanes // 2), f32),
            jax.ShapeDtypeStruct((2,), f32),
        ),
        in_specs=[pl.BlockSpec(memory_space=pl.ANY)] * 2,
        out_specs=(vmem, vmem, pl.BlockSpec(memory_space=pltpu.SMEM)),
        scratch_shapes=scratch,
        compiler_params=pltpu.CompilerParams(collective_id=0, has_side_effects=True),
    )(force, modulus)
    smem = pl.BlockSpec(memory_space=pltpu.SMEM)
    return pl.pallas_call(
        hand_out,
        out_shape=tuple(jax.ShapeDtypeStruct(v.shape, f32) for v in results),
        in_specs=(vmem, vmem, smem),
        out_specs=(pl.BlockSpec(memory_space=pl.ANY), pl.BlockSpec(memory_space=pl.ANY), smem),
        scratch_shapes=[pltpu.SemaphoreType.DMA((2,))],
    )(*results)


def solution(mesh):
    return jax.shard_map(
        functools.partial(body, mesh.shape["slab"]),
        mesh=mesh,
        in_specs=(P(None, "slab", None, "sample"), P("slab", None, "sample")),
        out_specs=(P(None, "slab", None, "sample"), P(None, "slab", None, "sample"), P("sample")),
        check_vma=False,
    )
```

```python
import functools

import jax
import jax.numpy as jnp
from jax import lax
from jax.experimental import pallas as pl
from jax.experimental.pallas import tpu as pltpu
from jax.sharding import PartitionSpec as P

CDEG = 4
FINE = (0.25, 2.0)
COARSE = (0.02, 2.0)
H = 8
REACH = 4
U_FINE = True
U_COARSE = True


def rounds(n):
    count = 0
    while REACH * 2**count < n - 1:
        count += 1
    return count


def coefficients(low, high, degree):
    centre, half = (high + low) / 2.0, (high - low) / 2.0
    ratio = centre / half
    rho = 1.0 / ratio
    steps = []
    for _ in range(degree - 1):
        nxt = 1.0 / (2.0 * ratio - rho)
        steps.append((nxt * rho, 2.0 * nxt / half))
        rho = nxt
    return 1.0 / centre, steps


def shifts(rows, lanes, step):
    lane = lax.broadcasted_iota(jnp.int32, (rows, lanes), 1)
    row = lax.broadcasted_iota(jnp.int32, (rows, lanes), 0)

    def ahead_x(u):
        return jnp.where(lane < lanes - step, pltpu.roll(u, lanes - step, 1), 0.0)

    def back_x(u):
        return jnp.where(lane >= step, pltpu.roll(u, step, 1), 0.0)

    def ahead_y(u):
        return jnp.where(row < rows - 1, pltpu.roll(u, rows - 1, 0), 0.0)

    def back_y(u):
        return jnp.where(row >= 1, pltpu.roll(u, 1, 0), 0.0)

    return ahead_x, back_x, ahead_y, back_y


def loop(lo, hi, body, carry, unroll):
    return lax.fori_loop(lo + H, hi + H, body, carry, unroll=unroll)


def invert(lam, inv, lo, hi, first, last, sh, unroll):
    _, back_x, _, back_y = sh

    def body(z, below):
        m = lam[z]
        mx, my = back_x(m), back_y(m)
        base = (m + below) + (m + my) + (m + mx) + m
        live = jnp.logical_and(z - H >= first, z - H < last)
        for c, extra in enumerate((mx, my, below)):
            inv[c, z] = jnp.where(live, 1.0 / (base + extra), 0.0)
        return m

    loop(lo, hi, body, lam[lo - 1 + H], unroll)


def parts_of(lo, hi, x, keep):
    if x is None or keep is None:
        return [(lo, hi, x)]
    return [(lo, keep[0], None), (keep[0], keep[1], x), (keep[1], hi, None)]


def begin(src, inv, w, x, lo, hi, scale, unroll, keep=None):
    def body(x, z, carry):
        for c in range(3):
            v = inv[c, z] * src[c, z] * scale
            w[c, z] = v
            if x is not None:
                x[c, z] = v
        return carry

    for a, b, kept in parts_of(lo, hi, x, keep):
        loop(a, b, functools.partial(body, kept), 0, unroll)


def sweep(src, r, w, x, lam, inv, lo, hi, old, new, sh, unroll, keep=None):
    ahead_x, back_x, ahead_y, back_y = sh

    def upward(z, u, div):
        m = lam[z]
        gz = [w[c, z + 1] - u[c] for c in range(3)]
        s = m * (div + gz[2])
        return [m * gz[0], m * gz[1], m * gz[2] + s], s, m

    def spread(u):
        return (ahead_x(u[0]) - u[0]) + (ahead_y(u[1]) - u[1])

    def body(x, z, below):
        u = [w[c, z] for c in range(3)]
        gx = [ahead_x(v) - v for v in u]
        gy = [ahead_y(v) - v for v in u]
        up, s, m = upward(z, u, gx[0] + gy[1])
        fx = [m * g for g in gx]
        fy = [m * g for g in gy]
        fx[0] = fx[0] + s
        fy[1] = fy[1] + s
        for c in range(3):
            a = (below[c] - up[c]) + (back_y(fy[c]) - fy[c]) + (back_x(fx[c]) - fx[c])
            rest = src[c, z] - a
            r[c, z] = rest
            if new is not None:
                v = new * (inv[c, z] * rest)
                if old is not None:
                    v = old * u[c] + v
                w[c, z] = v
                if x is not None:
                    x[c, z] = x[c, z] + v
        return tuple(up)

    z0 = lo - 1 + H
    u0 = [w[c, z0] for c in range(3)]
    up0, _, _ = upward(z0, u0, spread(u0))
    carry = tuple(up0)
    for a, b, kept in parts_of(lo, hi, x, keep):
        if a < b:
            carry = loop(a, b, functools.partial(body, kept), carry, unroll)


def pack(load, tmp, scale, even):
    lanes = even.shape[1]
    halves = []
    for k in range(2):
        tmp[k] = load(2 * k) + load(2 * k + 1)
        n = even.shape[0]
        halves.append(tmp[k, pl.ds(0, n, stride=2), :] + tmp[k, pl.ds(1, n, stride=2), :])
    a, b = halves
    return scale * jnp.where(even, a + pltpu.roll(a, lanes - 1, 1), b + pltpu.roll(b, 1, 1))


def unpack(p, even):
    lanes = even.shape[1]
    return jnp.where(even, p, pltpu.roll(p, 1, 1)), jnp.where(even, pltpu.roll(p, lanes - 1, 1), p)


def kernel(n, L, force, modulus, out, cout, comp, fm, lam, inv, r, w, x, tmp, cg, c1, c2, clam, cinv, cf, cr, cw, ce, part, known, cpart, lsem, ssem, rsem, sums_s, sums_r):
    me = lax.axis_index("slab")
    rows, lanes = fm.shape[2], fm.shape[3]
    crows = rows // 2
    barrier = pltpu.get_barrier_semaphore()

    def inside(i):
        return jnp.logical_and(i >= 0, i < n)

    def signal(sem, d):
        @pl.when(inside(me + d))
        def _():
            pl.semaphore_signal(sem, inc=1, device_id={"slab": me + d}, device_id_type=pl.DeviceIdType.MESH)

    greeted = 0
    for k in range(1, REACH + 1):
        for d in (k, -k):
            signal(barrier, d)
            greeted = greeted + inside(me + d).astype(jnp.int32)

    def round_tell(j):
        signal(known.at[2 * j], REACH * 2**j)
        signal(known.at[2 * j + 1], -REACH * 2**j)

    def round_hear(j):
        pl.when(inside(me - REACH * 2**j))(lambda: pl.semaphore_wait(known.at[2 * j], 1))
        pl.when(inside(me + REACH * 2**j))(lambda: pl.semaphore_wait(known.at[2 * j + 1], 1))

    own = pl.ds(H, L)
    loads = [
        pltpu.make_async_copy(force, fm.at[pl.ds(0, 3), own], lsem.at[0]),
        pltpu.make_async_copy(modulus, fm.at[3, own], lsem.at[1]),
    ]
    for cp in loads:
        cp.start()

    copies = {}

    def remote(name, src, dst, d):
        i = len(copies)
        copies[name] = (
            pltpu.make_async_remote_copy(
                src_ref=src, dst_ref=dst, send_sem=ssem.at[i], recv_sem=rsem.at[i],
                device_id={"slab": me + d}, device_id_type=pl.DeviceIdType.MESH,
            ),
            d, dst,
        )

    def start(name):
        cp, d, _ = copies[name]
        pl.when(inside(me + d))(cp.start)

    def wait(name):
        cp, d, _ = copies[name]
        pl.when(inside(me - d))(cp.wait_recv)

    def clear(name):
        _, d, dst = copies[name]

        @pl.when(jnp.logical_not(inside(me - d)))
        def _():
            dst[...] = jnp.zeros(dst.shape, jnp.float32)

    def layers(name, d, part, lo, hi):
        mine = fm.at[part, pl.ds(H + lo, hi - lo)]
        theirs = fm.at[part, pl.ds(H + lo - d * L, hi - lo)]
        remote(name, mine, theirs, d)

    force3, both = pl.ds(0, 3), pl.ds(0, 4)
    layers("near+", 1, force3, 2, L)
    layers("near+m", 1, 3, 1, L)
    layers("near-", -1, both, 0, 2)
    layers("next+", 1, force3, 0, 2)
    layers("next+m", 1, 3, 0, 1)
    layers("next-", -1, both, 2, L)
    layers("far+", 2, force3, 1, L)
    layers("far+m", 2, 3, 0, L)
    layers("far-", -2, both, 0, L - 1)
    for k in range(2, REACH + 1):
        for d in (k, -k):
            remote(("m", d), cg.at[4, 3], cg.at[4 - d, 3], d)
            remote(("g", d), cg.at[4, pl.ds(0, 3)], cg.at[4 - d, pl.ds(0, 3)], d)
    for name, buf, reach in (("c1", c1, 3), ("c2", c2, 2)):
        for k in range(1, reach + 1):
            for d in (k, -k):
                remote((name, d), buf.at[reach], buf.at[reach - d], d)

    for name in copies:
        clear(name)

    even = lax.rem(lax.broadcasted_iota(jnp.int32, (crows, lanes), 1), 2) == 0
    fsh = shifts(rows, lanes, 1)
    csh = shifts(crows, lanes, 2)
    fscale, ((fold, fnew),) = coefficients(*FINE, 2)
    cscale, csteps = coefficients(*COARSE, CDEG)
    _, wsteps = coefficients(*COARSE, 2 * CDEG)

    near = ("near+", "near+m", "near-")
    rest = ("next+", "next+m", "next-")
    far = ("far+", "far+m", "far-")
    for cp in loads:
        cp.wait()
    pl.semaphore_wait(barrier, greeted)
    round_tell(0)
    for name in near:
        start(name)
    for name in rest:
        start(name)

    def reduced(d, parts):
        for c in parts:
            cg[4 + d, c] = pack(lambda z: fm[c, H + d * L + z], tmp, 0.5 if c < 3 else 0.05, even)

    reduced(0, range(4))
    for k in range(2, REACH + 1):
        start(("m", k))
        start(("m", -k))
    for name in far:
        start(name)

    def take(lo, hi):
        def body(z, carry):
            lam[z] = 0.4 * fm[3, z]
            return carry

        loop(lo, hi, body, 0, U_FINE)

    first, last = -me * L, (n - me) * L
    cfirst, clast = -me * (L // 2), (n - me) * (L // 2)

    def exchange(name, buf, reach):
        for c in range(3):
            buf[reach, c] = pack(lambda z: r[c, H + z], tmp, 0.5, even)
        for k in range(1, reach + 1):
            start((name, k))
            start((name, -k))

    def gather(name, buf, reach, into):
        for k in range(1, reach + 1):
            wait((name, k))
            wait((name, -k))
        for d in range(-reach, reach + 1):
            for c in range(3):
                a, b = unpack(buf[reach + d, c], even)
                into[c, H + 2 * d] = a
                into[c, H + 2 * d + 1] = b

    for name in near:
        wait(name)
    take(-3, L + 2)
    invert(lam, inv, -2, L + 2, first, last, fsh, U_FINE)
    begin(fm, inv, w, None, -2, L + 2, fscale, U_FINE)
    sweep(fm, r, w, None, lam, inv, -1, L + 1, fold, fnew, fsh, U_FINE)
    sweep(r, r, w, None, lam, inv, 0, L, None, None, fsh, U_FINE)
    exchange("c1", c1, 3)
    for k in range(2, REACH + 1):
        start(("g", k))
        start(("g", -k))

    def solve(lo, hi, rhs, steps):
        begin(rhs, cinv, cw, ce, lo, hi, cscale, U_COARSE)
        for k, (old, new) in enumerate(steps):
            src = rhs if k == 0 else cr
            sweep(src, cr, cw, ce, clam, cinv, lo + k + 1, hi - k - 1, old, new, csh, U_COARSE)

    def prolong(lo, hi):
        def body(x, z, carry):
            for c in range(3):
                e = ce[c, z]
                for half in range(2):
                    f = 2 * (z - H) + half + H
                    w[c, f, pl.ds(0, crows, stride=2), :] = e
                    w[c, f, pl.ds(1, crows, stride=2), :] = e
                    if x is not None:
                        x[c, f] = x[c, f] + w[c, f]
            return carry

        for a, b, kept in parts_of(lo, hi, x, (0, L // 2)):
            loop(a, b, functools.partial(body, kept), 0, U_COARSE)

    for name in rest:
        wait(name)
    def spread_out(parts):
        for d in range(-REACH, REACH + 1):
            for c in parts:
                a, b = unpack(cg[4 + d, c], even)
                for z, v in ((H + 2 * d, a), (H + 2 * d + 1, b)):
                    if c < 3:
                        cf[c, z] = v
                    else:
                        clam[z] = v

    reduced(-1, (3,))
    reduced(1, (3,))
    for k in range(2, REACH + 1):
        wait(("m", k))
        wait(("m", -k))
    spread_out((3,))
    invert(clam, cinv, -7, 9, cfirst, clast, csh, U_COARSE)
    gather("c1", c1, 3, cr)
    solve(-6, 8, cr, csteps)

    for name in far:
        wait(name)
    take(-8, -3)
    take(L + 2, L + 7)
    invert(lam, inv, -7, -2, first, last, fsh, U_FINE)
    invert(lam, inv, L + 2, L + 7, first, last, fsh, U_FINE)
    begin(fm, inv, w, x, -7, L + 7, fscale, U_FINE, (0, L))
    sweep(fm, r, w, x, lam, inv, -6, L + 6, fold, fnew, fsh, U_FINE, (0, L))
    sweep(r, r, w, None, lam, inv, -5, L + 5, None, None, fsh, U_FINE)

    prolong(-3, 5)
    sweep(r, r, w, x, lam, inv, -5, L + 5, None, fscale, fsh, U_FINE, (0, L))
    sweep(r, r, w, x, lam, inv, -4, L + 4, fold, fnew, fsh, U_FINE, (0, L))
    sweep(r, r, w, x, lam, inv, -3, L + 3, None, fscale, fsh, U_FINE, (0, L))
    sweep(r, r, w, x, lam, inv, -2, L + 2, fold, fnew, fsh, U_FINE, (0, L))
    sweep(r, r, w, None, lam, inv, -1, L + 1, None, None, fsh, U_FINE)
    exchange("c2", c2, 2)

    for j in range(1, rounds(n)):
        round_hear(j - 1)
        round_tell(j)

    reduced(-1, range(3))
    reduced(1, range(3))
    for k in range(2, REACH + 1):
        wait(("g", k))
        wait(("g", -k))
    spread_out(range(3))
    solve(-7, 9, cf, wsteps)
    coarse_sum = jnp.zeros((crows, lanes), jnp.float32)
    pick = (
        lax.broadcasted_iota(jnp.int32, (lanes, lanes // 2), 0)
        == 2 * lax.broadcasted_iota(jnp.int32, (lanes, lanes // 2), 1)
    ).astype(jnp.float32)
    for c in range(3):
        for z in range(L // 2):
            v = ce[c, H + z]
            coarse_sum = coarse_sum + v * cf[c, H + z]
            cpart[c, z] = jnp.dot(v, pick, precision=lax.Precision.HIGHEST, preferred_element_type=jnp.float32)

    coarse_out = pltpu.make_async_copy(cpart, cout, lsem.at[2])
    coarse_out.start()

    gather("c2", c2, 2, cr)
    solve(-4, 6, cr, csteps)
    prolong(-1, 3)
    sweep(r, r, w, x, lam, inv, -1, L + 1, None, fscale, fsh, U_FINE, (0, L))
    sweep(r, r, w, x, lam, inv, 0, L, fold, fnew, fsh, U_FINE, (0, L))

    fine_sum = jnp.zeros((rows, lanes), jnp.float32)
    for c in range(3):
        for z in range(L):
            fine_sum = fine_sum + x[c, H + z] * fm[c, H + z]
    part[0, 0:1] = jnp.sum(fine_sum, axis=0, keepdims=True)
    part[0, 1:2] = jnp.sum(coarse_sum, axis=0, keepdims=True)

    fine_out = pltpu.make_async_copy(x.at[:, own], out, lsem.at[3])

    def tell(k):
        return pltpu.make_async_remote_copy(
            src_ref=part.at[0], dst_ref=part.at[k], send_sem=sums_s.at[k], recv_sem=sums_r.at[k],
            device_id={"slab": lax.rem(me + k, n)}, device_id_type=pl.DeviceIdType.MESH,
        )

    def say(k, carry):
        tell(k).start()
        return carry

    def hear(k, carry):
        tell(k).wait_recv()
        return carry

    round_hear(rounds(n) - 1)
    lax.fori_loop(1, n, say, 0)
    fine_out.start()
    for name in copies:
        cp, d, _ = copies[name]
        pl.when(inside(me + d))(cp.wait_send)
    lax.fori_loop(1, n, hear, 0)
    total = jnp.sum(part[...], axis=0)
    cells = 1.0 / (n * L * rows * lanes)
    comp[0] = jnp.sum(total[0:1]) * cells
    comp[1] = jnp.sum(total[1:2]) * cells

    def done(k, carry):
        tell(k).wait_send()
        return carry

    lax.fori_loop(1, n, done, 0)
    coarse_out.wait()
    fine_out.wait()


def hand_out(fine, coarse, comp, fine_out, coarse_out, comp_out, sem):
    copies = [pltpu.make_async_copy(fine, fine_out, sem.at[0]), pltpu.make_async_copy(coarse, coarse_out, sem.at[1])]
    for cp in copies:
        cp.start()
    for i in range(2):
        comp_out[i] = comp[i]
    for cp in copies:
        cp.wait()


def body(n, force, modulus):
    _, L, rows, lanes = force.shape
    f32 = jnp.float32
    fine, coarse = (L + 2 * H, rows, lanes), (L // 2 + 2 * H, rows // 2, lanes)
    pair = (rows // 2, lanes)
    V = pltpu.VMEM
    remotes = 9 + 6 + 6 + 6 + 4
    scratch = [
        V((4,) + fine, f32), V(fine, f32), V((3,) + fine, f32), V((3,) + fine, f32),
        V((3,) + fine, f32), V((3,) + fine, f32), V((2, rows, lanes), f32),
        V((9, 4) + pair, f32), V((7, 3) + pair, f32), V((5, 3) + pair, f32),
        V(coarse, f32), V((3,) + coarse, f32), V((3,) + coarse, f32), V((3,) + coarse, f32),
        V((3,) + coarse, f32), V((3,) + coarse, f32), V((n, 2, lanes), f32),
        pltpu.SemaphoreType.REGULAR((2 * rounds(n),)),
        V((3, L // 2, rows // 2, lanes // 2), f32),
        pltpu.SemaphoreType.DMA((4,)),
        pltpu.SemaphoreType.DMA((remotes,)), pltpu.SemaphoreType.DMA((remotes,)),
        pltpu.SemaphoreType.DMA((n,)), pltpu.SemaphoreType.DMA((n,)),
    ]
    vmem = pl.BlockSpec(memory_space=pltpu.VMEM)
    results = pl.pallas_call(
        functools.partial(kernel, n, L),
        out_shape=(
            jax.ShapeDtypeStruct(force.shape, f32),
            jax.ShapeDtypeStruct((3, L // 2, rows // 2, lanes // 2), f32),
            jax.ShapeDtypeStruct((2,), f32),
        ),
        in_specs=[pl.BlockSpec(memory_space=pl.ANY)] * 2,
        out_specs=(pl.BlockSpec(memory_space=pl.ANY), pl.BlockSpec(memory_space=pl.ANY), pl.BlockSpec(memory_space=pltpu.SMEM)),
        scratch_shapes=scratch,
        compiler_params=pltpu.CompilerParams(collective_id=0, has_side_effects=True),
    )(force, modulus)
    smem = pl.BlockSpec(memory_space=pltpu.SMEM)
    return pl.pallas_call(
        hand_out,
        out_shape=tuple(jax.ShapeDtypeStruct(v.shape, f32) for v in results),
        in_specs=(vmem, vmem, smem),
        out_specs=(pl.BlockSpec(memory_space=pl.ANY), pl.BlockSpec(memory_space=pl.ANY), smem),
        scratch_shapes=[pltpu.SemaphoreType.DMA((2,))],
    )(*results)


def solution(mesh):
    return jax.shard_map(
        functools.partial(body, mesh.shape["slab"]),
        mesh=mesh,
        in_specs=(P(None, "slab", None, "sample"), P("slab", None, "sample")),
        out_specs=(P(None, "slab", None, "sample"), P(None, "slab", None, "sample"), P("sample")),
        check_vma=False,
    )
```
